32 devices in a mesh: parts: 2 (over x), wide: 16 (over z, y, core).
Axes of the slice: x: 2, y: 2, z: 4, core: 2. Of those that a mesh axis runs over, the one named last changes fastest.
Arguments:
- voxels: bfloat16 [32768, 256], P(('parts', 'wide')), parts along dimension 0, may hold values from -16 to 16
- regular_window: int32 [32768], P(('parts', 'wide')), parts along dimension 0, may hold values from 0 to 127, never falling along the last dimension, each value on 1 to 256 neighbouring positions
- shifted_window: int32 [32768], P(('parts', 'wide')), parts along dimension 0, may hold values from 0 to 127, never falling along the last dimension, each value on 1 to 256 neighbouring positions
- dest: int32 [32768], P(('parts', 'wide')), parts along dimension 0, may hold values from 0 to 16383, as said below
- w_qkv: bfloat16 [2, 256, 768], replicated, may hold values from -0.375 to 0.375
- w_out: bfloat16 [2, 256, 256], replicated, may hold values from -1.5 to 1.5
- gain: float32 [2, 256], replicated, may hold values from 0.1 to 1.9
- temper: float32 [2, 8], replicated, may hold values from 0.5 to 6
Outputs:
- shifted_out: bfloat16 [32768, 256], P(('parts', 'wide')), parts along dimension 0
The draws below stay inside these ranges and needn't reach their ends.
There are 2 independent parts, one for each index of `parts`. The reference program is written for one: setup_inputs(seed, part) draws one part's arguments, and reference() takes and returns one part's arrays. A program takes and returns all parts, laid end to end along the dimension named above; an argument that names none is the same for every part. Nothing has to cross between parts.
Inputs may be any that keep to these rules, and one draw needn't show every extreme that they name: `regular_window`: window ids never fall along the order; every window has 1 to 256 voxels and one has exactly 256. `shifted_window`: window ids never fall along the order; every window has 1 to 256 voxels and one has exactly 256. dest is a permutation. Counting blocks of 1024 consecutive positions, at most 128 voxels go from one block of the regular order to one block of the shifted order, and some pair reaches 128; the count from a block to the block k places further along, cyclically, is the same for every block.
All inputs are finite; a program needn't handle non-finite values.
Results may differ from the reference program's by a relative error of at most 0.007.
The reference program's roundings to bfloat16 on the way (of `projected`, `weights`, `attended`, `sublayer`, `first` and `moved`) count: a program that leaves them out, or rounds other values in their place, can miss the bound.
Values may be sent and summed in bfloat16 or wider, within the bound.
A program may use at most 64 MiB of HBM per device.

```python
import math
import jax
import jax.numpy as jnp
import numpy as np
from jax import lax

C = 256
HEADS = 8
VOX_DEV = 1024
WIN = 256
VOXELS = 16384
WINDOWS = 128


def draw_voxels(key, part):
    first_key = jax.random.fold_in(key, 0)
    base = jax.random.normal(first_key, (VOXELS, C), jnp.float32)
    values = jnp.clip(base, -6.0, 6.0)
    return values.astype(jnp.bfloat16)


def draw_temper(key, part):
    uniforms = jax.random.uniform(key, (2, HEADS), jnp.float32)
    values = jnp.exp(math.log(0.5) + uniforms * math.log(8.0))
    return values.astype(jnp.float32)


def draw_dest(key, part):
    groups = VOXELS // VOX_DEV
    share = VOX_DEV // groups
    first_key, second_key, third_key, fourth_key = jax.random.split(key, 4)
    lifts = jax.random.randint(first_key, (groups // 2,), 0, share + 1).astype(jnp.int32)
    lifts = lifts.at[0].set(share)
    amounts = jnp.stack([share + lifts, share - lifts], axis=1).reshape(groups)
    amounts = amounts[jax.random.permutation(second_key, groups)]
    bounds = jnp.cumsum(amounts).astype(jnp.int32)
    local_order = jax.vmap(lambda one_key: jax.random.permutation(one_key, VOX_DEV))(jax.random.split(third_key, groups))
    local_order = local_order.astype(jnp.int32)
    offsets = jnp.sum((bounds[None, None, :] <= local_order[:, :, None]).astype(jnp.int32), axis=2)
    target = (jnp.arange(groups, dtype=jnp.int32)[:, None] + offsets) % groups
    arrival = jax.vmap(lambda one_key: jax.random.permutation(one_key, VOX_DEV))(jax.random.split(fourth_key, groups))
    arrival = arrival.astype(jnp.int32)
    final_slot = arrival[target, local_order]
    return (target * VOX_DEV + final_slot).reshape(VOXELS).astype(jnp.int32)


def profile(count, total, reach, slope):
    weights = [(1 << 20) // math.isqrt(standing ** slope) + 1 for standing in range(2, count + 1)]
    spare, counts = total - reach - (count - 1), [1] * (count - 1)
    while spare > 0:
        movable = [i for i in range(count - 1) if counts[i] < reach]
        whole, budget = sum([weights[i] for i in movable]), spare
        for i in movable:
            extra = min(reach - counts[i], max(1, budget * weights[i] // whole), spare)
            counts[i] = counts[i] + extra
            spare = spare - extra
    return np.array([reach] + counts)


def uneven_parts(own_key, number_of, total, bound, lean):
    if number_of == 2:
        one = jax.random.randint(own_key, (), max(1, total - bound), min(bound, total - 1) + 1)
        return jnp.stack([one, total - one])
    tallies = jnp.asarray(profile(number_of, total, bound, lean), jnp.int32)
    pairs = (number_of - 1) // 2
    source_of, sink = tallies[1:1 + 2 * pairs:2], tallies[2:2 + 2 * pairs:2]
    room = jnp.minimum(source_of - 1, bound - sink)
    shifted = jax.random.randint(jax.random.fold_in(own_key, 1), (pairs,), 0, 1 << 20) % (room + 1)
    tallies = tallies.at[1:1 + 2 * pairs:2].set(source_of - shifted).at[2:2 + 2 * pairs:2].set(sink + shifted)
    return tallies[jax.random.permutation(jax.random.fold_in(own_key, 2), number_of)]


def centred(key, dims, width, bound, kind=jnp.bfloat16):
    return jnp.clip(width * jax.random.normal(key, dims, jnp.float32), -bound, bound).astype(kind)


def setup_inputs(seed: int = 0, part: int = 0) -> dict:
    keys = jax.random.split(jax.random.key(seed), 9)
    part_keys = jax.random.split(jax.random.fold_in(keys[8], part), 9)
    voxels = draw_voxels(jax.random.fold_in(jax.random.fold_in(keys[8], part), 71), part)
    regular_window = jnp.searchsorted(jnp.cumsum(uneven_parts(part_keys[1], WINDOWS, VOXELS, WIN, 1)), jnp.arange(VOXELS), side="right").astype(jnp.int32)
    shifted_window = jnp.searchsorted(jnp.cumsum(uneven_parts(part_keys[2], WINDOWS, VOXELS, WIN, 1)), jnp.arange(VOXELS), side="right").astype(jnp.int32)
    dest = draw_dest(jax.random.fold_in(jax.random.fold_in(keys[8], part), 71), part)
    w_qkv = centred(keys[4], (2, C, 3 * C), C ** -0.5, 0.375)
    w_out = centred(keys[5], (2, C, C), (C // 16) ** -0.5, 1.5)
    gain = jnp.clip(1.0 + 0.18 * jax.random.normal(keys[6], (2, C), jnp.float32), 0.1, 1.9)
    temper = draw_temper(jax.random.fold_in(keys[8], 71), part)
    return {"voxels": voxels, "regular_window": regular_window, "shifted_window": shifted_window, "dest": dest, "w_qkv": w_qkv, "w_out": w_out, "gain": gain, "temper": temper}


epsilon = 1e-05
masked_score = -1e+30

def settle(hidden, attended, w_out_layer, gain_layer):
    summed = hidden.astype(jnp.float32) + jnp.dot(attended, w_out_layer, preferred_element_type=jnp.float32)
    center = lax.optimization_barrier(jnp.mean(summed, axis=1, keepdims=True))
    spread = lax.optimization_barrier(jnp.mean(jnp.square(summed - center), axis=1, keepdims=True))
    return ((summed - center) * lax.rsqrt(spread + epsilon) * gain_layer).astype(jnp.bfloat16)

def sublayer(hidden, window_ids, w_qkv_layer, w_out_layer, gain_layer, temper_layer):
    total_rows = hidden.shape[0]
    channels = hidden.shape[1]
    head_dim = channels // HEADS
    projected = jnp.dot(hidden, w_qkv_layer, preferred_element_type=jnp.float32).astype(jnp.bfloat16)
    queries = projected[:, :channels]
    padded = jnp.pad(projected[:, channels:], ((WIN, WIN), (0, 0)))
    marks = (window_ids + 1).astype(jnp.int32)
    marks_pad = jnp.pad(marks, (WIN, WIN))
    factor = temper_layer * (1.0 / math.sqrt(head_dim))
    block_rows = math.gcd(total_rows, 512)
    key_rows = block_rows + 2 * WIN

    def one_block(number):
        first_row = (number * block_rows).astype(jnp.int32)
        query_block = lax.dynamic_slice_in_dim(queries, first_row, block_rows, 0).astype(jnp.float32)
        query_block = query_block.reshape(block_rows, HEADS, head_dim)
        key_block = lax.dynamic_slice_in_dim(padded, first_row, key_rows, 0).astype(jnp.float32)
        keys_part = key_block[:, :channels].reshape(key_rows, HEADS, head_dim)
        values_part = key_block[:, channels:].reshape(key_rows, HEADS, head_dim)
        mark_query = lax.dynamic_slice_in_dim(marks, first_row, block_rows, 0)
        mark_key = lax.dynamic_slice_in_dim(marks_pad, first_row, key_rows, 0)
        same_window = (mark_query[:, None] == mark_key[None, :])[None]
        scores = jnp.einsum('qhd,khd->hqk', query_block, keys_part) * factor[:, None, None]
        scores = jnp.where(same_window, scores, masked_score)
        highest = lax.optimization_barrier(jnp.max(scores, axis=2, keepdims=True))
        exponents = jnp.where(same_window, jnp.exp(scores - highest), 0.0)
        totals = lax.optimization_barrier(jnp.sum(exponents, axis=2, keepdims=True))
        weights = (exponents / totals).astype(jnp.bfloat16)
        result = jnp.einsum('hqk,khd->qhd', weights.astype(jnp.float32), values_part)
        return result.reshape(block_rows, channels).astype(jnp.bfloat16)
    attended = lax.map(one_block, jnp.arange(total_rows // block_rows, dtype=jnp.int32))
    attended = attended.reshape(total_rows, channels)
    return settle(hidden, attended, w_out_layer, gain_layer)

def reference(voxels, regular_window, shifted_window, dest, w_qkv, w_out, gain, temper):
    first = sublayer(voxels, regular_window, w_qkv[0], w_out[0], gain[0], temper[0])
    moved = jnp.zeros_like(first).at[dest.astype(jnp.int32)].set(first)
    return sublayer(moved, shifted_window, w_qkv[1], w_out[1], gain[1], temper[1])
```

```python
import functools
import math

import jax
import jax.numpy as jnp
from jax import lax
from jax.experimental import pallas as pl
from jax.experimental.pallas import tpu as pltpu
from jax.sharding import PartitionSpec as P

HEADS = 8
LANES = 128
GROUPS = 2
ONES = 16
UNROLL = 2
SLOTS = 4

epsilon = 1e-05
apart = 2.0**100

BF = jnp.bfloat16
F32 = jnp.float32
NT = (((1,), (1,)), ((), ()))


def bit_flags(marks_row):
    count = marks_row.shape[1]
    place = lax.broadcasted_iota(jnp.int32, (LANES, count), 0)
    bit = (jnp.broadcast_to(marks_row, (LANES, count)) >> (place & 31)) & 1
    return jnp.where(place < LANES // 2, bit, 1 - bit).astype(F32)


def project_keys(h, marks_row, w, k_ref, code_ref, v_ref, first, q_ref=None, flag_ref=None):
    rows, channels = h.shape
    half = channels // GROUPS
    pair = v_ref.shape[1] - ONES
    start = 0 if q_ref is not None else channels
    qkv = jnp.dot(h, w[:, start:], preferred_element_type=F32)
    kv = qkv[:, channels - start :]
    flags = bit_flags(marks_row)
    at = pl.ds(first, rows)
    code_ref[at, :] = jnp.transpose((flags - 1.0) * apart).astype(BF)
    for g in range(GROUPS):
        k_ref[g, at, :] = kv[:, g * half : (g + 1) * half].astype(BF)
    turned = jnp.transpose(kv[:, channels:]).astype(BF)
    for t in range(v_ref.shape[0]):
        v_ref[t, :pair, at] = turned[t * pair : (t + 1) * pair]
    if q_ref is not None:
        own = pl.ds(first - rows, rows)
        q_ref[:, own] = jnp.transpose(qkv[:, :channels]).astype(BF)
        flag_ref[:, own] = flags.astype(BF)


def whole_kernel(
    n, temper_hbm, h_hbm, regular_hbm, shifted_hbm, dest_hbm, w_hbm, wo_hbm, gain_hbm, out_ref,
    temper_ref, h_ref, marks_ref, dest_ref, w_ref, wo_ref, gain_ref, load_sem,
    k_ref, code_ref, v_ref, q_ref, flag_ref, fac_ref, s_ref, att_ref,
    first_ref, moved_ref, low_ref, high_ref, mlow_ref, mhigh_ref,
    outgoing, arrived, slots_out, slots_in, halo_send, halo_recv, slot_send, slot_recv, row_send, row_recv,
):
    rows, channels = h_ref.shape
    rim = rows // 4
    block = rim
    capacity = outgoing.shape[1]
    half = channels // GROUPS
    head_dim = channels // HEADS
    tiles = v_ref.shape[0]
    heads_in = HEADS // tiles
    side = half
    key_rows = side + 2 * rim
    me = lax.axis_index("wide")
    right, left = lax.rem(me + 1, n), lax.rem(me + n - 1, n)

    barrier = pltpu.get_barrier_semaphore()

    def greet(t, carry):
        pl.semaphore_signal(
            barrier, inc=1, device_id={"wide": lax.rem(me + t, n)}, device_id_type=pl.DeviceIdType.MESH
        )
        return carry

    lax.fori_loop(1, n, greet, 0)

    loads = [
        pltpu.make_async_copy(src, dst, load_sem.at[number])
        for number, (src, dst) in enumerate(
            (
                (dest_hbm, dest_ref),
                (h_hbm, h_ref),
                (w_hbm, w_ref),
                (regular_hbm, marks_ref.at[0]),
                (shifted_hbm, marks_ref.at[1]),
                (temper_hbm, temper_ref),
                (gain_hbm, gain_ref),
                (wo_hbm, wo_ref),
            )
        )
    ]
    for load in loads:
        load.start()

    def remote(src, dst, send, recv, peer):
        return pltpu.make_async_remote_copy(
            src_ref=src, dst_ref=dst, send_sem=send, recv_sem=recv,
            device_id={"wide": peer}, device_id_type=pl.DeviceIdType.MESH,
        )

    v_ref[:, v_ref.shape[1] - ONES :, :] = jnp.ones((tiles, ONES, v_ref.shape[2]), BF)
    loads[0].wait()
    dest = dest_ref[...]
    target = lax.div(dest, jnp.full_like(dest, rows))
    slot = dest - target * rows + 1
    member = lax.broadcasted_iota(jnp.int32, (n, rows), 0) == jnp.broadcast_to(target, (n, rows))
    member = member.astype(F32)
    upper = (
        lax.broadcasted_iota(jnp.int32, (block, block), 0) <= lax.broadcasted_iota(jnp.int32, (block, block), 1)
    ).astype(F32).astype(BF)
    carry = jnp.zeros((n, 1), F32)
    ranks = []
    for r in range(0, rows, block):
        part = member[:, r : r + block]
        ranks.append(jnp.dot(part.astype(BF), upper, preferred_element_type=F32) + carry)
        carry = carry + jnp.sum(part, axis=1, keepdims=True)
    rank = jnp.sum(jnp.concatenate(ranks, axis=1) * member, axis=0, keepdims=True)
    position = rank.astype(jnp.int32) - 1
    width = slots_out.shape[2]
    chosen = (
        lax.broadcasted_iota(jnp.int32, (width, rows), 0) == jnp.broadcast_to(position, (width, rows))
    ).astype(F32).astype(BF)
    coarse = (member * (slot >> 5).astype(F32)).astype(BF)
    fine = (member * (slot & 31).astype(F32)).astype(BF)
    table = lax.dot_general(coarse, chosen, NT, preferred_element_type=F32) * 32.0
    table = (table + lax.dot_general(fine, chosen, NT, preferred_element_type=F32)).astype(jnp.int32)
    for t in range(n):
        slots_out[t] = table[t : t + 1, :]

    for load in loads[1:]:
        load.wait()
    factor = temper_ref[...] * (1.0 / math.sqrt(head_dim)) * math.log2(math.e)
    lane_head = lax.broadcasted_iota(jnp.int32, (1, heads_in * side), 1) // side
    for layer in range(2):
        for t in range(tiles):
            spread = jnp.broadcast_to(factor[layer : layer + 1, t * heads_in : t * heads_in + 1], lane_head.shape)
            for j in range(1, heads_in):
                other = factor[layer : layer + 1, t * heads_in + j : t * heads_in + j + 1]
                spread = jnp.where(lane_head == j, jnp.broadcast_to(other, lane_head.shape), spread)
            fac_ref[layer, t : t + 1, :] = spread

    def own_keys(layer, source, r):
        project_keys(
            source[r : r + block, :], marks_ref[layer, :, r : r + block], w_ref[layer],
            k_ref, code_ref, v_ref, rim + r, q_ref, flag_ref,
        )

    for r in range(0, rows, block):
        own_keys(0, h_ref, r)

    pl.semaphore_wait(barrier, n - 1)

    early = (
        (h_ref.at[pl.ds(0, rim)], high_ref.at[0], 0, left),
        (h_ref.at[pl.ds(rows - rim, rim)], low_ref.at[0], 1, right),
        (marks_ref.at[:, :, pl.ds(0, rim)], mhigh_ref, 2, left),
        (marks_ref.at[:, :, pl.ds(rows - rim, rim)], mlow_ref, 3, right),
    )
    late = (
        (moved_ref.at[pl.ds(0, rim)], high_ref.at[1], 4, left),
        (moved_ref.at[pl.ds(rows - rim, rim)], low_ref.at[1], 5, right),
    )

    def rim_copy(entry):
        src, dst, number, peer = entry
        return remote(src, dst, halo_send.at[number], halo_recv.at[number], peer)

    for entry in early:
        rim_copy(entry).start()

    def slot_copy(peer, source):
        return remote(slots_out.at[peer], slots_in.at[source], slot_send.at[peer], slot_recv.at[source], peer)

    def send_slots(t, carry):
        slot_copy(lax.rem(me + t, n), me).start()
        return carry

    lax.fori_loop(1, n, send_slots, 0)
    slots_in[me] = slots_out[me]

    row_head = lax.broadcasted_iota(jnp.int32, (half, heads_in * side), 0) // head_dim
    col_head = lax.broadcasted_iota(jnp.int32, (half, heads_in * side), 1) // side
    pair_rows = heads_in * head_dim
    cuts = [(a, min(a + 2 * LANES, key_rows)) for a in range(0, key_rows, 2 * LANES)]

    def attend_blocks(layer, where, count):
        per = tiles // GROUPS
        exact = layer == 0

        def queries(r, t):
            g, p = divmod(t, per)
            q = jnp.concatenate([q_ref[g * half : (g + 1) * half, pl.ds(r, side)]] * heads_in, axis=1)
            q = jnp.where(row_head == col_head + p * heads_in, q, jnp.zeros_like(q))
            flags = jnp.concatenate([flag_ref[:, pl.ds(r, side)]] * heads_in, axis=1)
            return jnp.concatenate([q, flags], axis=0)

        def score(wanted, r, t, a, b, tops):
            keys = pl.ds(r + a, b - a)
            lhs = jnp.concatenate([k_ref[t // per, keys, :], code_ref[keys, :]], axis=1)
            s = jnp.dot(lhs, wanted, preferred_element_type=F32)
            s_ref[t % SLOTS, a:b, :] = s
            s = jnp.max(s.reshape((b - a) // 8, 8, s.shape[1]), axis=0)
            return s if tops is None else jnp.maximum(tops, s)

        def emit(total, scale, r, t):
            for j in range(heads_in):
                own = slice(j * side, (j + 1) * side)
                o = total[j * head_dim : (j + 1) * head_dim, own]
                row = t * pair_rows + j * head_dim
                att_ref[row : row + head_dim, pl.ds(r, side)] = o if scale is None else o * scale[:, own]

        def values(e, r, t, a, b, total):
            keys = pl.ds(pl.multiple_of(r + a, LANES), b - a)
            part = jnp.dot(v_ref[t, :, keys], e, preferred_element_type=F32)
            return part if total is None else total + part

        def raised(t, a, b, top):
            return jnp.exp2((s_ref[t % SLOTS, a:b, :] - top) * fac_ref[layer, t : t + 1, :])

        def weighed(r, t, a, b, scale, total):
            return values((s_ref[t % SLOTS, a:b, :] * scale).astype(BF), r, t, a, b, total)

        def one(i, carry):
            tops, scale = carry
            r = pl.multiple_of(where(i) * side, side)
            after = pl.multiple_of(where(lax.rem(i + 1, count)) * side, side)
            before = pl.multiple_of(where(lax.rem(i + count - 1, count)) * side, side)
            for t in range(tiles):
                coming, r_coming = (t + 1, r) if t + 1 < tiles else (0, after)
                past, r_past = (t - 1, r) if t > 0 else (tiles - 1, before)
                wanted = queries(r_coming, coming)
                top = jnp.max(tops, axis=0, keepdims=True)
                total, tops, sums = None, None, None
                for a, b in cuts:
                    tops = score(wanted, r_coming, coming, a, b, tops)
                    e = raised(t, a, b, top)
                    if exact:
                        s_ref[t % SLOTS, a:b, :] = e
                        e = jnp.sum(e.reshape((b - a) // 8, 8, e.shape[1]), axis=0)
                        sums = e if sums is None else sums + e
                        total = weighed(r_past, past, a, b, scale, total)
                    else:
                        total = values(e.astype(BF), r, t, a, b, total)
                if exact:
                    emit(total, None, r_past, past)
                    scale = 1.0 / jnp.sum(sums, axis=0, keepdims=True)
                else:
                    emit(total, 1.0 / total[pair_rows : pair_rows + 1, :], r, t)
            return tops, scale

        r = pl.multiple_of(where(0) * side, side)
        wanted, tops = queries(r, 0), None
        for a, b in cuts:
            tops = score(wanted, r, 0, a, b, tops)
        scale = jnp.zeros((1, heads_in * side), F32)
        tops, scale = lax.fori_loop(0, count, one, (tops, scale), unroll=UNROLL)
        if exact:
            r, total = pl.multiple_of(where(count - 1) * side, side), None
            for a, b in cuts:
                total = weighed(r, tiles - 1, a, b, scale, total)
            emit(total, None, r, tiles - 1)

    def settle(layer, source, store, r):
        attended = jnp.transpose(att_ref[:, r : r + block]).astype(BF)
        summed = source[r : r + block, :].astype(F32)
        summed = summed + jnp.dot(attended, wo_ref[layer], preferred_element_type=F32)
        center = jnp.mean(summed, axis=1, keepdims=True)
        shifted = summed - center
        spread = jnp.mean(jnp.square(shifted), axis=1, keepdims=True)
        store[r : r + block, :] = (shifted * lax.rsqrt(spread + epsilon) * gain_ref[layer : layer + 1, :]).astype(BF)

    inside = (rows - 2 * rim) // side
    outside = 2 * rim // side

    def inner_half(layer, source, store):
        attend_blocks(layer, lambda i: i + rim // side, inside)
        for r in range(rim, rows - rim, block):
            settle(layer, source, store, r)

    def outer_half(layer, source, store):
        attend_blocks(layer, lambda i: i + i // (rim // side) * inside, outside)
        settle(layer, source, store, 0)
        settle(layer, source, store, rows - block)

    def layer_rims(layer):
        project_keys(low_ref[layer], mlow_ref[layer], w_ref[layer], k_ref, code_ref, v_ref, 0)
        project_keys(high_ref[layer], mhigh_ref[layer], w_ref[layer], k_ref, code_ref, v_ref, rim + rows)

    inner_half(0, h_ref, first_ref)
    for entry in early:
        rim_copy(entry).wait()
    layer_rims(0)
    outer_half(0, h_ref, first_ref)

    first = first_ref[...]
    place = lax.broadcasted_iota(jnp.int32, (capacity, rows), 0)

    def gathered(peer):
        wanted = jnp.where(target == peer, position, -1)
        pick = (place == jnp.broadcast_to(wanted, (capacity, rows))).astype(F32).astype(BF)
        return jnp.dot(pick, first, preferred_element_type=F32).astype(BF)

    def peer_at(t):
        odd = lax.rem(t, 2)
        return lax.rem(me + n // 2 + (2 * odd - 1) * ((t + 1) // 2) + n, n)

    def row_copy(peer, source):
        return remote(outgoing.at[peer], arrived.at[source], row_send.at[peer], row_recv.at[source], peer)

    outgoing[peer_at(0)] = gathered(peer_at(0))

    def exchange(t, carry):
        peer = peer_at(t)
        outgoing[peer] = gathered(peer)
        row_copy(peer_at(t - 1), me).start()
        return carry

    lax.fori_loop(1, n - 1, exchange, 0)
    arrived[me] = gathered(me)
    row_copy(peer_at(n - 2), me).start()

    def settle_copies(t, carry):
        other = lax.rem(me + t, n)
        slot_copy(other, other).wait()
        row_copy(other, other).wait()
        return carry

    lax.fori_loop(1, n, settle_copies, 0)

    places = jnp.concatenate([slots_in[t][:, :capacity] for t in range(n)], axis=1)
    came = arrived[...].reshape(n * capacity, channels)

    def land(r):
        here = lax.broadcasted_iota(jnp.int32, (block, n * capacity), 0) + (r + 1)
        pick = (here == jnp.broadcast_to(places, (block, n * capacity))).astype(F32).astype(BF)
        moved_ref[r : r + block, :] = jnp.dot(pick, came, preferred_element_type=F32).astype(BF)

    land(0)
    land(rows - block)
    land(block)
    for entry in late:
        rim_copy(entry).start()
    land(2 * block)
    for r in range(0, rows, block):
        own_keys(1, moved_ref, r)
    inner_half(1, moved_ref, out_ref)
    for entry in late:
        rim_copy(entry).wait()
    layer_rims(1)
    outer_half(1, moved_ref, out_ref)


def body(voxels, regular_window, shifted_window, dest, w_qkv, w_out, gain, temper):
    rows, channels = voxels.shape
    n = lax.axis_size("wide")
    rim = rows // 4
    half = channels // GROUPS
    capacity = 2 * rows // n
    tiles = HEADS // 2
    pair = channels // tiles
    keys = rows + 2 * rim
    vmem = pltpu.VMEM
    hbm = pl.BlockSpec(memory_space=pltpu.HBM)
    dma = pltpu.SemaphoreType.DMA
    return pl.pallas_call(
        functools.partial(whole_kernel, n),
        out_shape=jax.ShapeDtypeStruct((rows, channels), BF),
        in_specs=[hbm] * 8,
        out_specs=pl.BlockSpec(memory_space=pltpu.VMEM),
        scratch_shapes=[
            vmem(temper.shape, F32),
            vmem((rows, channels), BF),
            vmem((2, 1, rows), jnp.int32),
            vmem((1, rows), jnp.int32),
            vmem(w_qkv.shape, BF),
            vmem(w_out.shape, BF),
            vmem(gain.shape, F32),
            dma((8,)),
            vmem((GROUPS, keys, half), BF),
            vmem((keys, LANES), BF),
            vmem((tiles, pair + ONES, keys), BF),
            vmem((channels, rows), BF),
            vmem((LANES, rows), BF),
            vmem((2, tiles, 2 * half), F32),
            vmem((SLOTS, half + 2 * rim, 2 * half), F32),
            vmem((channels, rows), F32),
            vmem((rows, channels), BF),
            vmem((rows, channels), BF),
            vmem((2, rim, channels), BF),
            vmem((2, rim, channels), BF),
            vmem((2, 1, rim), jnp.int32),
            vmem((2, 1, rim), jnp.int32),
            vmem((n, capacity, channels), BF),
            vmem((n, capacity, channels), BF),
            vmem((n, 1, max(capacity, LANES)), jnp.int32),
            vmem((n, 1, max(capacity, LANES)), jnp.int32),
            dma((6,)), dma((6,)), dma((n,)), dma((n,)), dma((n,)), dma((n,)),
        ],
        compiler_params=pltpu.CompilerParams(
            vmem_limit_bytes=60 << 20, collective_id=0, has_side_effects=True
        ),
    )(
        temper, voxels, regular_window[None, :], shifted_window[None, :], dest[None, :], w_qkv, w_out, gain
    )


def solution(mesh):
    spread = P(("parts", "wide"))
    wide_rows = P(("parts", "wide"), None)
    return jax.shard_map(
        body,
        mesh=mesh,
        in_specs=(wide_rows, spread, spread, spread, P(), P(), P(), P()),
        out_specs=wide_rows,
        check_vma=False,
    )
```

```python
import functools
import math

import jax
import jax.numpy as jnp
from jax import lax
from jax.experimental import pallas as pl
from jax.experimental.pallas import tpu as pltpu
from jax.sharding import PartitionSpec as P

HEADS = 8
LANES = 128
GROUPS = 2
ONES = 16
UNROLL = 2
SLOTS = 4
STRIP = 64

epsilon = 1e-05
apart = 2.0**100

BF = jnp.bfloat16
F32 = jnp.float32
NT = (((1,), (1,)), ((), ()))


def bit_flags(marks_row):
    count = marks_row.shape[1]
    place = lax.broadcasted_iota(jnp.int32, (LANES, count), 0)
    bit = (jnp.broadcast_to(marks_row, (LANES, count)) >> (place & 31)) & 1
    return jnp.where(place < LANES // 2, bit, 1 - bit).astype(F32)


def project_keys(h, marks_row, w, k_ref, code_ref, v_ref, first, q_ref=None, flag_ref=None):
    rows, channels = h.shape
    half = channels // GROUPS
    pair = v_ref.shape[1] - ONES
    start = 0 if q_ref is not None else channels
    qkv = jnp.dot(h, w[:, start:], preferred_element_type=F32)
    kv = qkv[:, channels - start :]
    flags = bit_flags(marks_row)
    at = pl.ds(first, rows)
    code_ref[at, :] = jnp.transpose((flags - 1.0) * apart).astype(BF)
    for g in range(GROUPS):
        k_ref[g, at, :] = kv[:, g * half : (g + 1) * half].astype(BF)
    turned = jnp.transpose(kv[:, channels:]).astype(BF)
    for t in range(v_ref.shape[0]):
        v_ref[t, :pair, at] = turned[t * pair : (t + 1) * pair]
    if q_ref is not None:
        own = pl.ds(first - rows, rows)
        q_ref[:, own] = jnp.transpose(qkv[:, :channels]).astype(BF)
        flag_ref[:, own] = flags.astype(BF)


def whole_kernel(
    n, temper_hbm, h_hbm, regular_hbm, shifted_hbm, dest_hbm, w_hbm, wo_hbm, gain_hbm, out_ref,
    temper_ref, h_ref, marks_ref, dest_ref, w_ref, wo_ref, gain_ref, load_sem,
    k_ref, code_ref, v_ref, q_ref, flag_ref, fac_ref, s_ref, att_ref,
    first_ref, moved_ref, low_ref, high_ref, mlow_ref, mhigh_ref,
    outgoing, arrived, pick_ref, sum_ref, slots_out, slots_in, halo_send, halo_recv, slot_send, slot_recv, row_send, row_recv,
):
    rows, channels = h_ref.shape
    rim = rows // 4
    block = rim
    capacity = outgoing.shape[1]
    half = channels // GROUPS
    head_dim = channels // HEADS
    tiles = v_ref.shape[0]
    heads_in = HEADS // tiles
    side = half
    key_rows = side + 2 * rim
    me = lax.axis_index("wide")
    right, left = lax.rem(me + 1, n), lax.rem(me + n - 1, n)

    def partner(step):
        away = n // 2 + (1 - 2 * lax.rem(step, 2)) * lax.div(step, 2)
        return lax.rem(me + away + n, n)

    barrier = pltpu.get_barrier_semaphore()

    def greet(t, carry):
        pl.semaphore_signal(
            barrier, inc=1, device_id={"wide": lax.rem(me + t, n)}, device_id_type=pl.DeviceIdType.MESH
        )
        return carry

    lax.fori_loop(1, n, greet, 0)

    loads = [
        pltpu.make_async_copy(src, dst, load_sem.at[number])
        for number, (src, dst) in enumerate(
            (
                (dest_hbm, dest_ref),
                (h_hbm, h_ref),
                (w_hbm, w_ref),
                (regular_hbm, marks_ref.at[0]),
                (shifted_hbm, marks_ref.at[1]),
                (temper_hbm, temper_ref),
                (gain_hbm, gain_ref),
                (wo_hbm, wo_ref),
            )
        )
    ]
    for load in loads:
        load.start()

    def remote(src, dst, send, recv, peer):
        return pltpu.make_async_remote_copy(
            src_ref=src, dst_ref=dst, send_sem=send, recv_sem=recv,
            device_id={"wide": peer}, device_id_type=pl.DeviceIdType.MESH,
        )

    v_ref[:, v_ref.shape[1] - ONES :, :] = jnp.ones((tiles, ONES, v_ref.shape[2]), BF)
    loads[0].wait()
    dest = dest_ref[...]
    target = lax.div(dest, jnp.full_like(dest, rows))
    slot = dest - target * rows + 1
    member = lax.broadcasted_iota(jnp.int32, (n, rows), 0) == jnp.broadcast_to(target, (n, rows))
    member = member.astype(F32)
    upper = (
        lax.broadcasted_iota(jnp.int32, (block, block), 0) <= lax.broadcasted_iota(jnp.int32, (block, block), 1)
    ).astype(F32).astype(BF)
    carry = jnp.zeros((n, 1), F32)
    ranks = []
    for r in range(0, rows, block):
        part = member[:, r : r + block]
        ranks.append(jnp.dot(part.astype(BF), upper, preferred_element_type=F32) + carry)
        carry = carry + jnp.sum(part, axis=1, keepdims=True)
    rank = jnp.sum(jnp.concatenate(ranks, axis=1) * member, axis=0, keepdims=True)
    position = rank.astype(jnp.int32) - 1
    width = slots_out.shape[2]
    chosen = (
        lax.broadcasted_iota(jnp.int32, (width, rows), 0) == jnp.broadcast_to(position, (width, rows))
    ).astype(F32).astype(BF)
    coarse = (member * (slot >> 5).astype(F32)).astype(BF)
    fine = (member * (slot & 31).astype(F32)).astype(BF)
    table = lax.dot_general(coarse, chosen, NT, preferred_element_type=F32) * 32.0
    table = (table + lax.dot_general(fine, chosen, NT, preferred_element_type=F32)).astype(jnp.int32)
    for t in range(n):
        slots_out[t] = table[t : t + 1, :]

    for load in loads[1:]:
        load.wait()
    factor = temper_ref[...] * (1.0 / math.sqrt(head_dim)) * math.log2(math.e)
    lane_head = lax.broadcasted_iota(jnp.int32, (1, heads_in * side), 1) // side
    for layer in range(2):
        for t in range(tiles):
            spread = jnp.broadcast_to(factor[layer : layer + 1, t * heads_in : t * heads_in + 1], lane_head.shape)
            for j in range(1, heads_in):
                other = factor[layer : layer + 1, t * heads_in + j : t * heads_in + j + 1]
                spread = jnp.where(lane_head == j, jnp.broadcast_to(other, lane_head.shape), spread)
            fac_ref[layer, t : t + 1, :] = spread

    def own_keys(layer, source, r):
        project_keys(
            source[r : r + block, :], marks_ref[layer, :, r : r + block], w_ref[layer],
            k_ref, code_ref, v_ref, rim + r, q_ref, flag_ref,
        )

    for r in range(0, rows, block):
        own_keys(0, h_ref, r)

    pl.semaphore_wait(barrier, n - 1)

    early = (
        (h_ref.at[pl.ds(0, rim)], high_ref.at[0], 0, left),
        (h_ref.at[pl.ds(rows - rim, rim)], low_ref.at[0], 1, right),
        (marks_ref.at[:, :, pl.ds(0, rim)], mhigh_ref, 2, left),
        (marks_ref.at[:, :, pl.ds(rows - rim, rim)], mlow_ref, 3, right),
    )
    late = (
        (moved_ref.at[pl.ds(0, rim)], high_ref.at[1], 4, left),
        (moved_ref.at[pl.ds(rows - rim, rim)], low_ref.at[1], 5, right),
    )

    def rim_copy(entry):
        src, dst, number, peer = entry
        return remote(src, dst, halo_send.at[number], halo_recv.at[number], peer)

    for entry in early:
        rim_copy(entry).start()

    def slot_copy(t):
        peer = partner(t)
        return remote(slots_out.at[peer], slots_in.at[t], slot_send.at[t], slot_recv.at[t], peer)

    def send_slots(t, carry):
        slot_copy(t).start()
        return carry

    lax.fori_loop(1, n, send_slots, 0)
    slots_in[0] = slots_out[me]

    row_head = lax.broadcasted_iota(jnp.int32, (half, heads_in * side), 0) // head_dim
    col_head = lax.broadcasted_iota(jnp.int32, (half, heads_in * side), 1) // side
    pair_rows = heads_in * head_dim

    def attend_blocks(layer, where, count):
        per = tiles // GROUPS
        exact = layer == 0
        cut = key_rows if exact else 3 * LANES
        cuts = [(a, min(a + cut, key_rows)) for a in range(0, key_rows, cut)]

        def queries(r, t):
            g, p = divmod(t, per)
            q = jnp.concatenate([q_ref[g * half : (g + 1) * half, pl.ds(r, side)]] * heads_in, axis=1)
            q = jnp.where(row_head == col_head + p * heads_in, q, jnp.zeros_like(q))
            flags = jnp.concatenate([flag_ref[:, pl.ds(r, side)]] * heads_in, axis=1)
            return jnp.concatenate([q, flags], axis=0)

        def score(wanted, r, t, a, b, tops):
            keys = pl.ds(r + a, b - a)
            lhs = jnp.concatenate([k_ref[t // per, keys, :], code_ref[keys, :]], axis=1)
            s = jnp.dot(lhs, wanted, preferred_element_type=F32)
            s_ref[t % SLOTS, a:b, :] = s
            s = jnp.max(s.reshape((b - a) // 8, 8, s.shape[1]), axis=0)
            return s if tops is None else jnp.maximum(tops, s)

        def emit(total, scale, r, t):
            for j in range(heads_in):
                own = slice(j * side, (j + 1) * side)
                o = total[j * head_dim : (j + 1) * head_dim, own]
                row = t * pair_rows + j * head_dim
                att_ref[row : row + head_dim, pl.ds(r, side)] = o if scale is None else o * scale[:, own]

        def values(e, r, t, a, b, total):
            keys = pl.ds(pl.multiple_of(r + a, LANES), b - a)
            part = jnp.dot(v_ref[t, :, keys], e, preferred_element_type=F32)
            return part if total is None else total + part

        def raised(t, a, b, top):
            return jnp.exp2((s_ref[t % SLOTS, a:b, :] - top) * fac_ref[layer, t : t + 1, :])

        def weighed(r, t, a, b, scale, total):
            return values((s_ref[t % SLOTS, a:b, :] * scale).astype(BF), r, t, a, b, total)

        def one(i, carry):
            tops, scale = carry
            r = pl.multiple_of(where(i) * side, side)
            after = pl.multiple_of(where(lax.rem(i + 1, count)) * side, side)
            before = pl.multiple_of(where(lax.rem(i + count - 1, count)) * side, side)
            for t in range(tiles):
                coming, r_coming = (t + 1, r) if t + 1 < tiles else (0, after)
                past, r_past = (t - 1, r) if t > 0 else (tiles - 1, before)
                wanted = queries(r_coming, coming)
                top = jnp.max(tops, axis=0, keepdims=True)
                total, tops, sums = None, None, None
                for a, b in cuts:
                    tops = score(wanted, r_coming, coming, a, b, tops)
                    if exact:
                        total = weighed(r_past, past, a, b, scale, total)
                        for c in range(a, b, STRIP):
                            e = raised(t, c, c + STRIP, top)
                            s_ref[t % SLOTS, c : c + STRIP, :] = e
                            e = jnp.sum(e.reshape(STRIP // 8, 8, e.shape[1]), axis=0)
                            sums = e if sums is None else sums + e
                    else:
                        total = values(raised(t, a, b, top).astype(BF), r, t, a, b, total)
                if exact:
                    emit(total, None, r_past, past)
                    scale = 1.0 / jnp.sum(sums, axis=0, keepdims=True)
                else:
                    emit(total, 1.0 / total[pair_rows : pair_rows + 1, :], r, t)
            return tops, scale

        r = pl.multiple_of(where(0) * side, side)
        wanted, tops = queries(r, 0), None
        for a, b in cuts:
            tops = score(wanted, r, 0, a, b, tops)
        scale = jnp.zeros((1, heads_in * side), F32)
        tops, scale = lax.fori_loop(0, count, one, (tops, scale), unroll=UNROLL)
        if exact:
            r, total = pl.multiple_of(where(count - 1) * side, side), None
            for a, b in cuts:
                total = weighed(r, tiles - 1, a, b, scale, total)
            emit(total, None, r, tiles - 1)

    def settle(layer, source, store, r):
        attended = jnp.transpose(att_ref[:, r : r + block]).astype(BF)
        summed = source[r : r + block, :].astype(F32)
        summed = summed + jnp.dot(attended, wo_ref[layer], preferred_element_type=F32)
        center = jnp.mean(summed, axis=1, keepdims=True)
        shifted = summed - center
        spread = jnp.mean(jnp.square(shifted), axis=1, keepdims=True)
        store[r : r + block, :] = (shifted * lax.rsqrt(spread + epsilon) * gain_ref[layer : layer + 1, :]).astype(BF)

    inside = (rows - 2 * rim) // side
    outside = 2 * rim // side

    def inner_half(layer, source, store):
        attend_blocks(layer, lambda i: i + rim // side, inside)
        for r in range(rim, rows - rim, block):
            settle(layer, source, store, r)

    def outer_half(layer, source, store):
        attend_blocks(layer, lambda i: i + i // (rim // side) * inside, outside)
        settle(layer, source, store, 0)
        settle(layer, source, store, rows - block)

    def layer_rims(layer):
        project_keys(low_ref[layer], mlow_ref[layer], w_ref[layer], k_ref, code_ref, v_ref, 0)
        project_keys(high_ref[layer], mhigh_ref[layer], w_ref[layer], k_ref, code_ref, v_ref, rim + rows)

    inner_half(0, h_ref, first_ref)
    for entry in early:
        rim_copy(entry).wait()
    layer_rims(0)
    outer_half(0, h_ref, first_ref)

    first = first_ref[...]
    place = lax.broadcasted_iota(jnp.int32, (capacity, rows), 0)

    def gathered(peer):
        wanted = jnp.where(target == peer, position, -1)
        pick = (place == jnp.broadcast_to(wanted, (capacity, rows))).astype(F32).astype(BF)
        return jnp.dot(pick, first, preferred_element_type=F32).astype(BF)

    def row_copy(t):
        return remote(outgoing.at[t], arrived.at[t], row_send.at[t], row_recv.at[t], partner(t))

    def exchange(t, carry):
        outgoing[t] = gathered(partner(t))
        row_copy(t).start()
        return carry

    lax.fori_loop(1, n, exchange, 0)
    arrived[0] = gathered(me)

    def settle_slots(t, carry):
        slot_copy(t).wait()
        return carry

    lax.fori_loop(1, n, settle_slots, 0)
    places = jnp.concatenate([slots_in[t][:, :capacity] for t in range(n)], axis=1)

    def prepare(i, carry):
        r = pl.multiple_of(i * block, block)
        here = lax.broadcasted_iota(jnp.int32, (block, n * capacity), 0) + (r + 1)
        pick_ref[pl.ds(r, block), :] = (here == jnp.broadcast_to(places, here.shape)).astype(F32).astype(BF)
        return carry

    lax.fori_loop(0, rows // block, prepare, 0)

    def settle_rows(t, carry):
        row_copy(t).wait()
        return carry

    quarter = n // 4
    groups = [(a * quarter, (a + 1) * quarter) for a in range(4)]

    def land(r, number):
        a, b = groups[number]
        came = arrived[a:b].reshape((b - a) * capacity, channels)
        part = jnp.dot(
            pick_ref[r : r + block, a * capacity : b * capacity], came, preferred_element_type=F32
        )
        if number > 0:
            part = part + sum_ref[r : r + block, :]
        if number + 1 < len(groups):
            sum_ref[r : r + block, :] = part
        else:
            moved_ref[r : r + block, :] = part.astype(BF)

    for number, (a, b) in enumerate(groups):
        lax.fori_loop(max(a, 1), b, settle_rows, 0)
        if number + 1 < len(groups):
            for r in range(0, rows, block):
                land(r, number)
    land(0, len(groups) - 1)
    land(rows - block, len(groups) - 1)
    for entry in late:
        rim_copy(entry).start()
    for r in range(block, rows - block, block):
        land(r, len(groups) - 1)
    for r in range(0, rows, block):
        own_keys(1, moved_ref, r)
    inner_half(1, moved_ref, out_ref)
    for entry in late:
        rim_copy(entry).wait()
    layer_rims(1)
    outer_half(1, moved_ref, out_ref)


def body(voxels, regular_window, shifted_window, dest, w_qkv, w_out, gain, temper):
    rows, channels = voxels.shape
    n = lax.axis_size("wide")
    rim = rows // 4
    half = channels // GROUPS
    capacity = 2 * rows // n
    tiles = HEADS // 2
    pair = channels // tiles
    keys = rows + 2 * rim
    vmem = pltpu.VMEM
    hbm = pl.BlockSpec(memory_space=pltpu.HBM)
    dma = pltpu.SemaphoreType.DMA
    return pl.pallas_call(
        functools.partial(whole_kernel, n),
        out_shape=jax.ShapeDtypeStruct((rows, channels), BF),
        in_specs=[hbm] * 8,
        out_specs=pl.BlockSpec(memory_space=pltpu.VMEM),
        scratch_shapes=[
            vmem(temper.shape, F32),
            vmem((rows, channels), BF),
            vmem((2, 1, rows), jnp.int32),
            vmem((1, rows), jnp.int32),
            vmem(w_qkv.shape, BF),
            vmem(w_out.shape, BF),
            vmem(gain.shape, F32),
            dma((8,)),
            vmem((GROUPS, keys, half), BF),
            vmem((keys, LANES), BF),
            vmem((tiles, pair + ONES, keys), BF),
            vmem((channels, rows), BF),
            vmem((LANES, rows), BF),
            vmem((2, tiles, 2 * half), F32),
            vmem((SLOTS, half + 2 * rim, 2 * half), F32),
            vmem((channels, rows), F32),
            vmem((rows, channels), BF),
            vmem((rows, channels), BF),
            vmem((2, rim, channels), BF),
            vmem((2, rim, channels), BF),
            vmem((2, 1, rim), jnp.int32),
            vmem((2, 1, rim), jnp.int32),
            vmem((n, capacity, channels), BF),
            vmem((n, capacity, channels), BF),
            vmem((rows, n * capacity), BF),
            vmem((rows, channels), F32),
            vmem((n, 1, max(capacity, LANES)), jnp.int32),
            vmem((n, 1, max(capacity, LANES)), jnp.int32),
            dma((6,)), dma((6,)), dma((n,)), dma((n,)), dma((n,)), dma((n,)),
        ],
        compiler_params=pltpu.CompilerParams(
            vmem_limit_bytes=53 << 20, collective_id=0, has_side_effects=True
        ),
    )(
        *(
            pltpu.with_memory_space_constraint(operand, pltpu.HBM)
            for operand in (
                temper, voxels, regular_window[None, :], shifted_window[None, :], dest[None, :], w_qkv, w_out, gain
            )
        )
    )


def solution(mesh):
    spread = P(("parts", "wide"))
    wide_rows = P(("parts", "wide"), None)
    return jax.shard_map(
        body,
        mesh=mesh,
        in_specs=(wide_rows, spread, spread, spread, P(), P(), P(), P()),
        out_specs=wide_rows,
        check_vma=False,
    )
```

```python
import functools
import math

import jax
import jax.numpy as jnp
from jax import lax
from jax.experimental import pallas as pl
from jax.experimental.pallas import tpu as pltpu
from jax.sharding import PartitionSpec as P

HEADS = 8
LANES = 128
GROUPS = 2
ONES = 16
UNROLL = 4
SLOTS = 4
STRIP = 64

epsilon = 1e-05
apart = 2.0**100

BF = jnp.bfloat16
F32 = jnp.float32
NT = (((1,), (1,)), ((), ()))


def bit_flags(marks_row):
    count = marks_row.shape[1]
    place = lax.broadcasted_iota(jnp.int32, (LANES, count), 0)
    bit = (jnp.broadcast_to(marks_row, (LANES, count)) >> (place & 31)) & 1
    return jnp.where((place & 32) == 0, bit, 1 - bit).astype(F32)


def project_keys(h, marks_row, w, k_ref, code_ref, v_ref, first, fac_row=None, q_ref=None, low_q_ref=None, flag_ref=None):
    rows, channels = h.shape
    half = channels // GROUPS
    pair = v_ref.shape[1] - ONES
    start = 0 if q_ref is not None else channels
    qkv = jnp.dot(h, w[:, start:], preferred_element_type=F32)
    kv = qkv[:, channels - start :]
    flags = bit_flags(marks_row)
    at = pl.ds(first, rows)
    code = jnp.transpose((flags - 1.0) * apart)
    lane_pair = lax.broadcasted_iota(jnp.int32, (rows, half), 1) // pair
    for g in range(GROUPS):
        keys = kv[:, g * half : (g + 1) * half]
        k_ref[g, at, :] = keys.astype(BF)
        for p in range(half // pair):
            code_ref[g * (half // pair) + p, at, :] = jnp.where(lane_pair == p, keys, code).astype(BF)
    turned = jnp.transpose(kv[:, channels:]).astype(BF)
    for t in range(v_ref.shape[0]):
        v_ref[t, :pair, at] = turned[t * pair : (t + 1) * pair]
    if q_ref is not None:
        own = pl.ds(first - rows, rows)
        q = jnp.transpose(qkv[:, :channels].astype(BF).astype(F32) * fac_row)
        high = q.astype(BF)
        q_ref[:, own] = high
        low_q_ref[:, own] = (q - high.astype(F32)).astype(BF)
        flag_ref[:, own] = flags.astype(BF)


def whole_kernel(
    n, temper_hbm, h_hbm, regular_hbm, shifted_hbm, dest_hbm, w_hbm, wo_hbm, gain_hbm, out_ref,
    temper_ref, h_ref, marks_ref, dest_ref, w_ref, wo_ref, gain_ref, load_sem,
    k_ref, code_ref, v_ref, q_ref, low_q_ref, flag_ref, fac_ref, s_ref, att_ref,
    first_ref, moved_ref, low_ref, high_ref, mlow_ref, mhigh_ref,
    outgoing, arrived, pick_ref, sum_ref, slots_out, slots_in, halo_send, halo_recv, slot_send, slot_recv, row_send, row_recv,
):
    rows, channels = h_ref.shape
    rim = rows // 4
    block = rim
    capacity = outgoing.shape[1]
    half = channels // GROUPS
    head_dim = channels // HEADS
    tiles = v_ref.shape[0]
    heads_in = HEADS // tiles
    side = half
    key_rows = side + 2 * rim
    me = lax.axis_index("wide")
    right, left = lax.rem(me + 1, n), lax.rem(me + n - 1, n)

    def partner(step):
        away = n // 2 + (1 - 2 * lax.rem(step, 2)) * lax.div(step, 2)
        return lax.rem(me + away + n, n)

    barrier = pltpu.get_barrier_semaphore()

    def greet(t, carry):
        pl.semaphore_signal(
            barrier, inc=1, device_id={"wide": lax.rem(me + t, n)}, device_id_type=pl.DeviceIdType.MESH
        )
        return carry

    lax.fori_loop(1, n, greet, 0)

    loads = [
        pltpu.make_async_copy(src, dst, load_sem.at[number])
        for number, (src, dst) in enumerate(
            (
                (dest_hbm, dest_ref),
                (h_hbm, h_ref),
                (w_hbm, w_ref),
                (regular_hbm, marks_ref.at[0]),
                (shifted_hbm, marks_ref.at[1]),
                (temper_hbm, temper_ref),
                (gain_hbm, gain_ref),
                (wo_hbm, wo_ref),
            )
        )
    ]
    for load in loads:
        load.start()

    def remote(src, dst, send, recv, peer):
        return pltpu.make_async_remote_copy(
            src_ref=src, dst_ref=dst, send_sem=send, recv_sem=recv,
            device_id={"wide": peer}, device_id_type=pl.DeviceIdType.MESH,
        )

    v_ref[:, v_ref.shape[1] - ONES :, :] = jnp.ones((tiles, ONES, v_ref.shape[2]), BF)
    loads[0].wait()
    dest = dest_ref[...]
    target = lax.div(dest, jnp.full_like(dest, rows))
    slot = dest - target * rows + 1
    member = lax.broadcasted_iota(jnp.int32, (n, rows), 0) == jnp.broadcast_to(target, (n, rows))
    member = member.astype(F32)
    upper = (
        lax.broadcasted_iota(jnp.int32, (block, block), 0) <= lax.broadcasted_iota(jnp.int32, (block, block), 1)
    ).astype(F32).astype(BF)
    carry = jnp.zeros((n, 1), F32)
    ranks = []
    for r in range(0, rows, block):
        part = member[:, r : r + block]
        ranks.append(jnp.dot(part.astype(BF), upper, preferred_element_type=F32) + carry)
        carry = carry + jnp.sum(part, axis=1, keepdims=True)
    rank = jnp.sum(jnp.concatenate(ranks, axis=1) * member, axis=0, keepdims=True)
    position = rank.astype(jnp.int32) - 1
    width = slots_out.shape[2]
    chosen = (
        lax.broadcasted_iota(jnp.int32, (width, rows), 0) == jnp.broadcast_to(position, (width, rows))
    ).astype(F32).astype(BF)
    coarse = (member * (slot >> 5).astype(F32)).astype(BF)
    fine = (member * (slot & 31).astype(F32)).astype(BF)
    table = lax.dot_general(coarse, chosen, NT, preferred_element_type=F32) * 32.0
    table = (table + lax.dot_general(fine, chosen, NT, preferred_element_type=F32)).astype(jnp.int32)
    for t in range(n):
        slots_out[t] = table[t : t + 1, :]

    for load in loads[1:]:
        load.wait()
    factor = temper_ref[...] * (1.0 / math.sqrt(head_dim)) * math.log2(math.e)
    lane_head = lax.broadcasted_iota(jnp.int32, (1, channels), 1) // head_dim
    for layer in range(2):
        spread = jnp.broadcast_to(factor[layer : layer + 1, 0:1], lane_head.shape)
        for j in range(1, HEADS):
            other = jnp.broadcast_to(factor[layer : layer + 1, j : j + 1], lane_head.shape)
            spread = jnp.where(lane_head == j, other, spread)
        fac_ref[layer : layer + 1, :] = spread

    def own_keys(layer, source, r):
        project_keys(
            source[r : r + block, :], marks_ref[layer, :, r : r + block], w_ref[layer],
            k_ref, code_ref, v_ref, rim + r, fac_ref[layer : layer + 1, :], q_ref, low_q_ref, flag_ref,
        )

    for r in range(0, rows, block):
        own_keys(0, h_ref, r)

    pl.semaphore_wait(barrier, n - 1)

    early = (
        (h_ref.at[pl.ds(0, rim)], high_ref.at[0], 0, left),
        (h_ref.at[pl.ds(rows - rim, rim)], low_ref.at[0], 1, right),
        (marks_ref.at[:, :, pl.ds(0, rim)], mhigh_ref, 2, left),
        (marks_ref.at[:, :, pl.ds(rows - rim, rim)], mlow_ref, 3, right),
    )
    late = (
        (moved_ref.at[pl.ds(0, rim)], high_ref.at[1], 4, left),
        (moved_ref.at[pl.ds(rows - rim, rim)], low_ref.at[1], 5, right),
    )

    def rim_copy(entry):
        src, dst, number, peer = entry
        return remote(src, dst, halo_send.at[number], halo_recv.at[number], peer)

    for entry in early:
        rim_copy(entry).start()

    def slot_copy(t):
        peer = partner(t)
        return remote(slots_out.at[peer], slots_in.at[t], slot_send.at[t], slot_recv.at[t], peer)

    def send_slots(t, carry):
        slot_copy(t).start()
        return carry

    lax.fori_loop(1, n, send_slots, 0)
    slots_in[0] = slots_out[me]

    row_head = lax.broadcasted_iota(jnp.int32, (half, heads_in * side), 0) // head_dim
    col_head = lax.broadcasted_iota(jnp.int32, (half, heads_in * side), 1) // side
    pair_rows = heads_in * head_dim

    def attend_blocks(layer, where, count):
        per = tiles // GROUPS
        exact = layer == 0
        cut = key_rows if exact else 3 * LANES
        cuts = [(a, min(a + cut, key_rows)) for a in range(0, key_rows, cut)]

        def queries(r, t):
            g, p = divmod(t, per)
            keep = row_head == col_head + p * heads_in
            group = slice(g * half, (g + 1) * half)

            def beside(ref, lanes):
                return jnp.concatenate([ref[lanes, pl.ds(r, side)]] * heads_in, axis=1)

            high = beside(q_ref, group)
            none = jnp.zeros_like(high)
            rest = jnp.where(row_head // heads_in == p, none, beside(flag_ref, slice(0, LANES)))
            return jnp.concatenate(
                [jnp.where(keep, high, none), jnp.where(keep, beside(low_q_ref, group), rest)], axis=0
            )

        def score(wanted, r, t, a, b, tops):
            keys = pl.ds(r + a, b - a)
            lhs = jnp.concatenate([k_ref[t // per, keys, :], code_ref[t, keys, :]], axis=1)
            s = jnp.dot(lhs, wanted, preferred_element_type=F32)
            s_ref[t % SLOTS, a:b, :] = s
            s = jnp.max(s.reshape((b - a) // 8, 8, s.shape[1]), axis=0)
            return s if tops is None else jnp.maximum(tops, s)

        def emit(total, scale, r, t):
            for j in range(heads_in):
                own = slice(j * side, (j + 1) * side)
                o = total[j * head_dim : (j + 1) * head_dim, own]
                row = t * pair_rows + j * head_dim
                att_ref[row : row + head_dim, pl.ds(r, side)] = o if scale is None else o * scale[:, own]

        def values(e, r, t, a, b, total):
            keys = pl.ds(pl.multiple_of(r + a, LANES), b - a)
            part = jnp.dot(v_ref[t, :, keys], e, preferred_element_type=F32)
            return part if total is None else total + part

        def raised(t, a, b, top):
            return jnp.exp2(s_ref[t % SLOTS, a:b, :] - top)

        def weighed(r, t, a, b, scale, total):
            return values((s_ref[t % SLOTS, a:b, :] * scale).astype(BF), r, t, a, b, total)

        def one(i, carry):
            tops, scale = carry
            r = pl.multiple_of(where(i) * side, side)
            after = pl.multiple_of(where(lax.rem(i + 1, count)) * side, side)
            before = pl.multiple_of(where(lax.rem(i + count - 1, count)) * side, side)
            for t in range(tiles):
                coming, r_coming = (t + 1, r) if t + 1 < tiles else (0, after)
                past, r_past = (t - 1, r) if t > 0 else (tiles - 1, before)
                wanted = queries(r_coming, coming)
                top = jnp.max(tops, axis=0, keepdims=True)
                total, tops, sums = None, None, None
                for a, b in cuts:
                    tops = score(wanted, r_coming, coming, a, b, tops)
                    if exact:
                        total = weighed(r_past, past, a, b, scale, total)
                        for c in range(a, b, STRIP):
                            e = raised(t, c, c + STRIP, top)
                            s_ref[t % SLOTS, c : c + STRIP, :] = e
                            e = jnp.sum(e.reshape(STRIP // 8, 8, e.shape[1]), axis=0)
                            sums = e if sums is None else sums + e
                    else:
                        total = values(raised(t, a, b, top).astype(BF), r, t, a, b, total)
                if exact:
                    emit(total, None, r_past, past)
                    scale = 1.0 / jnp.sum(sums, axis=0, keepdims=True)
                else:
                    emit(total, 1.0 / total[pair_rows : pair_rows + 1, :], r, t)
            return tops, scale

        r = pl.multiple_of(where(0) * side, side)
        wanted, tops = queries(r, 0), None
        for a, b in cuts:
            tops = score(wanted, r, 0, a, b, tops)
        scale = jnp.zeros((1, heads_in * side), F32)
        tops, scale = lax.fori_loop(0, count, one, (tops, scale), unroll=UNROLL)
        if exact:
            r, total = pl.multiple_of(where(count - 1) * side, side), None
            for a, b in cuts:
                total = weighed(r, tiles - 1, a, b, scale, total)
            emit(total, None, r, tiles - 1)

    def settle(layer, source, store, r):
        attended = jnp.transpose(att_ref[:, r : r + block]).astype(BF)
        summed = source[r : r + block, :].astype(F32)
        summed = summed + jnp.dot(attended, wo_ref[layer], preferred_element_type=F32)
        center = jnp.mean(summed, axis=1, keepdims=True)
        shifted = summed - center
        spread = jnp.mean(jnp.square(shifted), axis=1, keepdims=True)
        store[r : r + block, :] = (shifted * lax.rsqrt(spread + epsilon) * gain_ref[layer : layer + 1, :]).astype(BF)

    inside = (rows - 2 * rim) // side
    outside = 2 * rim // side

    def inner_half(layer, source, store):
        attend_blocks(layer, lambda i: i + rim // side, inside)
        for r in range(rim, rows - rim, block):
            settle(layer, source, store, r)

    def outer_half(layer, source, store):
        attend_blocks(layer, lambda i: i + i // (rim // side) * inside, outside)
        settle(layer, source, store, 0)
        settle(layer, source, store, rows - block)

    def layer_rims(layer):
        project_keys(low_ref[layer], mlow_ref[layer], w_ref[layer], k_ref, code_ref, v_ref, 0)
        project_keys(high_ref[layer], mhigh_ref[layer], w_ref[layer], k_ref, code_ref, v_ref, rim + rows)

    inner_half(0, h_ref, first_ref)
    for entry in early:
        rim_copy(entry).wait()
    layer_rims(0)
    outer_half(0, h_ref, first_ref)

    first = first_ref[...]
    place = lax.broadcasted_iota(jnp.int32, (capacity, rows), 0)

    def gathered(peer):
        wanted = jnp.where(target == peer, position, -1)
        pick = (place == jnp.broadcast_to(wanted, (capacity, rows))).astype(F32).astype(BF)
        return jnp.dot(pick, first, preferred_element_type=F32).astype(BF)

    def row_copy(t):
        return remote(outgoing.at[t], arrived.at[t], row_send.at[t], row_recv.at[t], partner(t))

    def exchange(t, carry):
        outgoing[t] = gathered(partner(t))
        row_copy(t).start()
        return carry

    lax.fori_loop(1, n, exchange, 0)
    arrived[0] = gathered(me)

    def settle_slots(t, carry):
        slot_copy(t).wait()
        return carry

    lax.fori_loop(1, n, settle_slots, 0)
    places = jnp.concatenate([slots_in[t][:, :capacity] for t in range(n)], axis=1)

    def prepare(i, carry):
        r = pl.multiple_of(i * block, block)
        here = lax.broadcasted_iota(jnp.int32, (block, n * capacity), 0) + (r + 1)
        pick_ref[pl.ds(r, block), :] = (here == jnp.broadcast_to(places, here.shape)).astype(F32).astype(BF)
        return carry

    lax.fori_loop(0, rows // block, prepare, 0)

    def settle_rows(t, carry):
        row_copy(t).wait()
        return carry

    quarter = n // 4
    groups = [(a * quarter, (a + 1) * quarter) for a in range(4)]

    def land(r, number):
        a, b = groups[number]
        came = arrived[a:b].reshape((b - a) * capacity, channels)
        part = jnp.dot(
            pick_ref[r : r + block, a * capacity : b * capacity], came, preferred_element_type=F32
        )
        if number > 0:
            part = part + sum_ref[r : r + block, :]
        if number + 1 < len(groups):
            sum_ref[r : r + block, :] = part
        else:
            moved_ref[r : r + block, :] = part.astype(BF)

    for number, (a, b) in enumerate(groups):
        lax.fori_loop(max(a, 1), b, settle_rows, 0)
        if number + 1 < len(groups):
            for r in range(0, rows, block):
                land(r, number)
    land(0, len(groups) - 1)
    land(rows - block, len(groups) - 1)
    for entry in late:
        rim_copy(entry).start()
    for r in range(block, rows - block, block):
        land(r, len(groups) - 1)
    for r in range(0, rows, block):
        own_keys(1, moved_ref, r)
    inner_half(1, moved_ref, out_ref)
    for entry in late:
        rim_copy(entry).wait()
    layer_rims(1)
    outer_half(1, moved_ref, out_ref)


def body(voxels, regular_window, shifted_window, dest, w_qkv, w_out, gain, temper):
    rows, channels = voxels.shape
    n = lax.axis_size("wide")
    rim = rows // 4
    half = channels // GROUPS
    capacity = 2 * rows // n
    tiles = HEADS // 2
    pair = channels // tiles
    keys = rows + 2 * rim
    vmem = pltpu.VMEM
    hbm = pl.BlockSpec(memory_space=pltpu.HBM)
    dma = pltpu.SemaphoreType.DMA
    return pl.pallas_call(
        functools.partial(whole_kernel, n),
        out_shape=jax.ShapeDtypeStruct((rows, channels), BF),
        in_specs=[hbm] * 8,
        out_specs=pl.BlockSpec(memory_space=pltpu.VMEM),
        scratch_shapes=[
            vmem(temper.shape, F32),
            vmem((rows, channels), BF),
            vmem((2, 1, rows), jnp.int32),
            vmem((1, rows), jnp.int32),
            vmem(w_qkv.shape, BF),
            vmem(w_out.shape, BF),
            vmem(gain.shape, F32),
            dma((8,)),
            vmem((GROUPS, keys, half), BF),
            vmem((tiles, keys, LANES), BF),
            vmem((tiles, pair + ONES, keys), BF),
            vmem((channels, rows), BF),
            vmem((channels, rows), BF),
            vmem((LANES, rows), BF),
            vmem((2, channels), F32),
            vmem((SLOTS, half + 2 * rim, 2 * half), F32),
            vmem((channels, rows), F32),
            vmem((rows, channels), BF),
            vmem((rows, channels), BF),
            vmem((2, rim, channels), BF),
            vmem((2, rim, channels), BF),
            vmem((2, 1, rim), jnp.int32),
            vmem((2, 1, rim), jnp.int32),
            vmem((n, capacity, channels), BF),
            vmem((n, capacity, channels), BF),
            vmem((rows, n * capacity), BF),
            vmem((rows, channels), F32),
            vmem((n, 1, max(capacity, LANES)), jnp.int32),
            vmem((n, 1, max(capacity, LANES)), jnp.int32),
            dma((6,)), dma((6,)), dma((n,)), dma((n,)), dma((n,)), dma((n,)),
        ],
        compiler_params=pltpu.CompilerParams(
            vmem_limit_bytes=53 << 20, collective_id=0, has_side_effects=True
        ),
    )(
        *(
            pltpu.with_memory_space_constraint(operand, pltpu.HBM)
            for operand in (
                temper, voxels, regular_window[None, :], shifted_window[None, :], dest[None, :], w_qkv, w_out, gain
            )
        )
    )


def solution(mesh):
    spread = P(("parts", "wide"))
    wide_rows = P(("parts", "wide"), None)
    return jax.shard_map(
        body,
        mesh=mesh,
        in_specs=(wide_rows, spread, spread, spread, P(), P(), P(), P()),
        out_specs=wide_rows,
        check_vma=False,
    )
```

```python
import functools
import math

import jax
import jax.numpy as jnp
from jax import lax
from jax.experimental import pallas as pl
from jax.experimental.pallas import tpu as pltpu
from jax.sharding import PartitionSpec as P

HEADS = 8
LANES = 128
GROUPS = 2
ONES = 16
UNROLL = 4
SLOTS = 4
STRIP = 64

epsilon = 1e-05
apart = 2.0**100

BF = jnp.bfloat16
F32 = jnp.float32
NT = (((1,), (1,)), ((), ()))


def bit_flags(marks_row):
    count = marks_row.shape[1]
    place = lax.broadcasted_iota(jnp.int32, (LANES, count), 0)
    bit = (jnp.broadcast_to(marks_row, (LANES, count)) >> (place & 31)) & 1
    return jnp.where((place & 32) == 0, bit, 1 - bit).astype(F32)


def project_keys(h, marks_row, w, k_ref, code_ref, v_ref, first, fac_row=None, q_ref=None, low_q_ref=None, flag_ref=None):
    rows, channels = h.shape
    half = channels // GROUPS
    pair = v_ref.shape[1] - ONES
    start = 0 if q_ref is not None else channels
    qkv = jnp.dot(h, w[:, start:], preferred_element_type=F32)
    kv = qkv[:, channels - start :]
    flags = bit_flags(marks_row)
    at = pl.ds(first, rows)
    code = jnp.transpose((flags - 1.0) * apart)
    lane_pair = lax.broadcasted_iota(jnp.int32, (rows, half), 1) // pair
    for g in range(GROUPS):
        keys = kv[:, g * half : (g + 1) * half]
        k_ref[g, at, :] = keys.astype(BF)
        for p in range(half // pair):
            code_ref[g * (half // pair) + p, at, :] = jnp.where(lane_pair == p, keys, code).astype(BF)
    turned = jnp.transpose(kv[:, channels:]).astype(BF)
    for t in range(v_ref.shape[0]):
        v_ref[t, :pair, at] = turned[t * pair : (t + 1) * pair]
    if q_ref is not None:
        own = pl.ds(first - rows, rows)
        q = jnp.transpose(qkv[:, :channels].astype(BF).astype(F32) * fac_row)
        high = q.astype(BF)
        q_ref[:, own] = high
        low_q_ref[:, own] = (q - high.astype(F32)).astype(BF)
        flag_ref[:, own] = flags.astype(BF)


def whole_kernel(
    n, temper_hbm, h_hbm, regular_hbm, shifted_hbm, dest_hbm, w_hbm, wo_hbm, gain_hbm, out_ref,
    temper_ref, h_ref, marks_ref, dest_ref, w_ref, wo_ref, gain_ref, load_sem,
    k_ref, code_ref, v_ref, q_ref, low_q_ref, flag_ref, fac_ref, s_ref, att_ref,
    first_ref, moved_ref, low_ref, high_ref, mlow_ref, mhigh_ref,
    outgoing, arrived, pick_ref, sum_ref, slots_out, slots_in, halo_send, halo_recv, slot_send, slot_recv, row_send, row_recv,
):
    rows, channels = h_ref.shape
    rim = rows // 4
    block = rim
    capacity = outgoing.shape[1]
    half = channels // GROUPS
    head_dim = channels // HEADS
    tiles = v_ref.shape[0]
    heads_in = HEADS // tiles
    side = half
    key_rows = side + 2 * rim
    me = lax.axis_index("wide")
    right, left = lax.rem(me + 1, n), lax.rem(me + n - 1, n)

    def partner(step):
        away = n // 2 + (1 - 2 * lax.rem(step, 2)) * lax.div(step, 2)
        return lax.rem(me + away + n, n)

    barrier = pltpu.get_barrier_semaphore()

    def greet(t, carry):
        pl.semaphore_signal(
            barrier, inc=1, device_id={"wide": lax.rem(me + t, n)}, device_id_type=pl.DeviceIdType.MESH
        )
        return carry

    lax.fori_loop(1, n, greet, 0)

    loads = [
        pltpu.make_async_copy(src, dst, load_sem.at[number])
        for number, (src, dst) in enumerate(
            (
                (dest_hbm, dest_ref),
                (h_hbm, h_ref),
                (w_hbm, w_ref),
                (regular_hbm, marks_ref.at[0]),
                (shifted_hbm, marks_ref.at[1]),
                (temper_hbm, temper_ref),
                (gain_hbm, gain_ref),
                (wo_hbm, wo_ref),
            )
        )
    ]
    for load in loads:
        load.start()

    def remote(src, dst, send, recv, peer):
        return pltpu.make_async_remote_copy(
            src_ref=src, dst_ref=dst, send_sem=send, recv_sem=recv,
            device_id={"wide": peer}, device_id_type=pl.DeviceIdType.MESH,
        )

    v_ref[:, v_ref.shape[1] - ONES :, :] = jnp.ones((tiles, ONES, v_ref.shape[2]), BF)
    loads[0].wait()
    dest = dest_ref[...]
    target = lax.div(dest, jnp.full_like(dest, rows))
    slot = dest - target * rows + 1
    member = lax.broadcasted_iota(jnp.int32, (n, rows), 0) == jnp.broadcast_to(target, (n, rows))
    member = member.astype(F32)
    upper = (
        lax.broadcasted_iota(jnp.int32, (block, block), 0) <= lax.broadcasted_iota(jnp.int32, (block, block), 1)
    ).astype(F32).astype(BF)
    carry = jnp.zeros((n, 1), F32)
    ranks = []
    for r in range(0, rows, block):
        part = member[:, r : r + block]
        ranks.append(jnp.dot(part.astype(BF), upper, preferred_element_type=F32) + carry)
        carry = carry + jnp.sum(part, axis=1, keepdims=True)
    rank = jnp.sum(jnp.concatenate(ranks, axis=1) * member, axis=0, keepdims=True)
    position = rank.astype(jnp.int32) - 1
    width = slots_out.shape[2]
    chosen = (
        lax.broadcasted_iota(jnp.int32, (width, rows), 0) == jnp.broadcast_to(position, (width, rows))
    ).astype(F32).astype(BF)
    coarse = (member * (slot >> 5).astype(F32)).astype(BF)
    fine = (member * (slot & 31).astype(F32)).astype(BF)
    table = lax.dot_general(coarse, chosen, NT, preferred_element_type=F32) * 32.0
    table = (table + lax.dot_general(fine, chosen, NT, preferred_element_type=F32)).astype(jnp.int32)
    for t in range(n):
        slots_out[t] = table[t : t + 1, :]

    for load in loads[1:]:
        load.wait()
    factor = temper_ref[...] * (1.0 / math.sqrt(head_dim)) * math.log2(math.e)
    lane_head = lax.broadcasted_iota(jnp.int32, (1, channels), 1) // head_dim
    for layer in range(2):
        spread = jnp.broadcast_to(factor[layer : layer + 1, 0:1], lane_head.shape)
        for j in range(1, HEADS):
            other = jnp.broadcast_to(factor[layer : layer + 1, j : j + 1], lane_head.shape)
            spread = jnp.where(lane_head == j, other, spread)
        fac_ref[layer : layer + 1, :] = spread

    def own_keys(layer, source, r):
        project_keys(
            source[r : r + block, :], marks_ref[layer, :, r : r + block], w_ref[layer],
            k_ref, code_ref, v_ref, rim + r, fac_ref[layer : layer + 1, :], q_ref, low_q_ref, flag_ref,
        )

    for r in range(0, rows, block):
        own_keys(0, h_ref, r)

    pl.semaphore_wait(barrier, n - 1)

    early = (
        (h_ref.at[pl.ds(0, rim)], high_ref.at[0], 0, left),
        (h_ref.at[pl.ds(rows - rim, rim)], low_ref.at[0], 1, right),
        (marks_ref.at[:, :, pl.ds(0, rim)], mhigh_ref, 2, left),
        (marks_ref.at[:, :, pl.ds(rows - rim, rim)], mlow_ref, 3, right),
    )
    late = (
        (moved_ref.at[pl.ds(0, rim)], high_ref.at[1], 4, left),
        (moved_ref.at[pl.ds(rows - rim, rim)], low_ref.at[1], 5, right),
    )

    def rim_copy(entry):
        src, dst, number, peer = entry
        return remote(src, dst, halo_send.at[number], halo_recv.at[number], peer)

    for entry in early:
        rim_copy(entry).start()

    def slot_copy(t):
        peer = partner(t)
        return remote(slots_out.at[peer], slots_in.at[t], slot_send.at[t], slot_recv.at[t], peer)

    def send_slots(t, carry):
        slot_copy(t).start()
        return carry

    lax.fori_loop(1, n, send_slots, 0)
    slots_in[0] = slots_out[me]

    row_head = lax.broadcasted_iota(jnp.int32, (half, heads_in * side), 0) // head_dim
    col_head = lax.broadcasted_iota(jnp.int32, (half, heads_in * side), 1) // side
    pair_rows = heads_in * head_dim

    def attend_blocks(layer, where, count):
        per = tiles // GROUPS
        exact = layer == 0
        cut = 3 * LANES
        cuts = [(a, min(a + cut, key_rows)) for a in range(0, key_rows, cut)]

        def queries(r, t):
            g, p = divmod(t, per)
            keep = row_head == col_head + p * heads_in
            group = slice(g * half, (g + 1) * half)

            def beside(ref, lanes):
                return jnp.concatenate([ref[lanes, pl.ds(r, side)]] * heads_in, axis=1)

            high = beside(q_ref, group)
            none = jnp.zeros_like(high)
            rest = jnp.where(row_head // heads_in == p, none, beside(flag_ref, slice(0, LANES)))
            return jnp.concatenate(
                [jnp.where(keep, high, none), jnp.where(keep, beside(low_q_ref, group), rest)], axis=0
            )

        def score(wanted, r, t, a, b, tops):
            keys = pl.ds(r + a, b - a)
            lhs = jnp.concatenate([k_ref[t // per, keys, :], code_ref[t, keys, :]], axis=1)
            s = jnp.dot(lhs, wanted, preferred_element_type=F32)
            s_ref[t % SLOTS, a:b, :] = s
            s = jnp.max(s.reshape((b - a) // 8, 8, s.shape[1]), axis=0)
            return s if tops is None else jnp.maximum(tops, s)

        def emit(total, scale, r, t):
            for j in range(heads_in):
                own = slice(j * side, (j + 1) * side)
                o = total[j * head_dim : (j + 1) * head_dim, own]
                row = t * pair_rows + j * head_dim
                att_ref[row : row + head_dim, pl.ds(r, side)] = o if scale is None else o * scale[:, own]

        def values(e, r, t, a, b, total):
            keys = pl.ds(pl.multiple_of(r + a, LANES), b - a)
            part = jnp.dot(v_ref[t, :, keys], e, preferred_element_type=F32)
            return part if total is None else total + part

        def raised(t, a, b, top):
            return jnp.exp2(s_ref[t % SLOTS, a:b, :] - top)

        def weighed(r, t, a, b, scale, total):
            return values((s_ref[t % SLOTS, a:b, :] * scale).astype(BF), r, t, a, b, total)

        def one(i, carry):
            tops, scale = carry
            r = pl.multiple_of(where(i) * side, side)
            after = pl.multiple_of(where(lax.rem(i + 1, count)) * side, side)
            before = pl.multiple_of(where(lax.rem(i + count - 1, count)) * side, side)
            for t in range(tiles):
                coming, r_coming = (t + 1, r) if t + 1 < tiles else (0, after)
                past, r_past = (t - 1, r) if t > 0 else (tiles - 1, before)
                wanted = queries(r_coming, coming)
                top = jnp.max(tops, axis=0, keepdims=True)
                total, tops, sums = None, None, None
                for a, b in cuts:
                    tops = score(wanted, r_coming, coming, a, b, tops)
                    if exact:
                        total = weighed(r_past, past, a, b, scale, total)
                        for c in range(a, b, STRIP):
                            e = raised(t, c, c + STRIP, top)
                            s_ref[t % SLOTS, c : c + STRIP, :] = e
                            e = jnp.sum(e.reshape(STRIP // 8, 8, e.shape[1]), axis=0)
                            sums = e if sums is None else sums + e
                    else:
                        total = values(raised(t, a, b, top).astype(BF), r, t, a, b, total)
                if exact:
                    emit(total, None, r_past, past)
                    scale = 1.0 / jnp.sum(sums, axis=0, keepdims=True)
                else:
                    emit(total, 1.0 / total[pair_rows : pair_rows + 1, :], r, t)
            return tops, scale

        r = pl.multiple_of(where(0) * side, side)
        wanted, tops = queries(r, 0), None
        for a, b in cuts:
            tops = score(wanted, r, 0, a, b, tops)
        scale = jnp.zeros((1, heads_in * side), F32)
        tops, scale = lax.fori_loop(0, count, one, (tops, scale), unroll=UNROLL)
        if exact:
            r, total = pl.multiple_of(where(count - 1) * side, side), None
            for a, b in cuts:
                total = weighed(r, tiles - 1, a, b, scale, total)
            emit(total, None, r, tiles - 1)

    def settle(layer, source, store, r):
        attended = jnp.transpose(att_ref[:, r : r + block]).astype(BF)
        summed = source[r : r + block, :].astype(F32)
        summed = summed + jnp.dot(attended, wo_ref[layer], preferred_element_type=F32)
        center = jnp.mean(summed, axis=1, keepdims=True)
        shifted = summed - center
        spread = jnp.mean(jnp.square(shifted), axis=1, keepdims=True)
        store[r : r + block, :] = (shifted * lax.rsqrt(spread + epsilon) * gain_ref[layer : layer + 1, :]).astype(BF)

    inside = (rows - 2 * rim) // side
    outside = 2 * rim // side

    def inner_half(layer, source, store):
        attend_blocks(layer, lambda i: i + rim // side, inside)
        for r in range(rim, rows - rim, block):
            settle(layer, source, store, r)

    def outer_half(layer, source, store):
        attend_blocks(layer, lambda i: i + i // (rim // side) * inside, outside)
        settle(layer, source, store, 0)
        settle(layer, source, store, rows - block)

    def layer_rims(layer):
        project_keys(low_ref[layer], mlow_ref[layer], w_ref[layer], k_ref, code_ref, v_ref, 0)
        project_keys(high_ref[layer], mhigh_ref[layer], w_ref[layer], k_ref, code_ref, v_ref, rim + rows)

    inner_half(0, h_ref, first_ref)
    for entry in early:
        rim_copy(entry).wait()
    layer_rims(0)
    outer_half(0, h_ref, first_ref)

    first = first_ref[...]
    place = lax.broadcasted_iota(jnp.int32, (capacity, rows), 0)

    def gathered(peer):
        wanted = jnp.where(target == peer, position, -1)
        pick = (place == jnp.broadcast_to(wanted, (capacity, rows))).astype(F32).astype(BF)
        return jnp.dot(pick, first, preferred_element_type=F32).astype(BF)

    def row_copy(t):
        return remote(outgoing.at[t], arrived.at[t], row_send.at[t], row_recv.at[t], partner(t))

    def exchange(t, carry):
        outgoing[t] = gathered(partner(t))
        row_copy(t).start()
        return carry

    lax.fori_loop(1, n, exchange, 0)
    arrived[0] = gathered(me)

    def settle_slots(t, carry):
        slot_copy(t).wait()
        return carry

    lax.fori_loop(1, n, settle_slots, 0)
    places = jnp.concatenate([slots_in[t][:, :capacity] for t in range(n)], axis=1)

    def prepare(i, carry):
        r = pl.multiple_of(i * block, block)
        here = lax.broadcasted_iota(jnp.int32, (block, n * capacity), 0) + (r + 1)
        pick_ref[pl.ds(r, block), :] = (here == jnp.broadcast_to(places, here.shape)).astype(F32).astype(BF)
        return carry

    lax.fori_loop(0, rows // block, prepare, 0)

    def settle_rows(t, carry):
        row_copy(t).wait()
        return carry

    quarter = n // 4
    groups = [(a * quarter, (a + 1) * quarter) for a in range(4)]

    def land(r, number):
        a, b = groups[number]
        came = arrived[a:b].reshape((b - a) * capacity, channels)
        part = jnp.dot(
            pick_ref[r : r + block, a * capacity : b * capacity], came, preferred_element_type=F32
        )
        if number > 0:
            part = part + sum_ref[r : r + block, :]
        if number + 1 < len(groups):
            sum_ref[r : r + block, :] = part
        else:
            moved_ref[r : r + block, :] = part.astype(BF)

    for number, (a, b) in enumerate(groups):
        lax.fori_loop(max(a, 1), b, settle_rows, 0)
        if number + 1 < len(groups):
            for r in range(0, rows, block):
                land(r, number)
    land(0, len(groups) - 1)
    land(rows - block, len(groups) - 1)
    for entry in late:
        rim_copy(entry).start()
    for r in range(block, rows - block, block):
        land(r, len(groups) - 1)
    for r in range(0, rows, block):
        own_keys(1, moved_ref, r)
    inner_half(1, moved_ref, out_ref)
    for entry in late:
        rim_copy(entry).wait()
    layer_rims(1)
    outer_half(1, moved_ref, out_ref)


def body(voxels, regular_window, shifted_window, dest, w_qkv, w_out, gain, temper):
    rows, channels = voxels.shape
    n = lax.axis_size("wide")
    rim = rows // 4
    half = channels // GROUPS
    capacity = 2 * rows // n
    tiles = HEADS // 2
    pair = channels // tiles
    keys = rows + 2 * rim
    vmem = pltpu.VMEM
    hbm = pl.BlockSpec(memory_space=pltpu.HBM)
    dma = pltpu.SemaphoreType.DMA
    return pl.pallas_call(
        functools.partial(whole_kernel, n),
        out_shape=jax.ShapeDtypeStruct((rows, channels), BF),
        in_specs=[hbm] * 8,
        out_specs=pl.BlockSpec(memory_space=pltpu.VMEM),
        scratch_shapes=[
            vmem(temper.shape, F32),
            vmem((rows, channels), BF),
            vmem((2, 1, rows), jnp.int32),
            vmem((1, rows), jnp.int32),
            vmem(w_qkv.shape, BF),
            vmem(w_out.shape, BF),
            vmem(gain.shape, F32),
            dma((8,)),
            vmem((GROUPS, keys, half), BF),
            vmem((tiles, keys, LANES), BF),
            vmem((tiles, pair + ONES, keys), BF),
            vmem((channels, rows), BF),
            vmem((channels, rows), BF),
            vmem((LANES, rows), BF),
            vmem((2, channels), F32),
            vmem((SLOTS, half + 2 * rim, 2 * half), F32),
            vmem((channels, rows), F32),
            vmem((rows, channels), BF),
            vmem((rows, channels), BF),
            vmem((2, rim, channels), BF),
            vmem((2, rim, channels), BF),
            vmem((2, 1, rim), jnp.int32),
            vmem((2, 1, rim), jnp.int32),
            vmem((n, capacity, channels), BF),
            vmem((n, capacity, channels), BF),
            vmem((rows, n * capacity), BF),
            vmem((rows, channels), F32),
            vmem((n, 1, max(capacity, LANES)), jnp.int32),
            vmem((n, 1, max(capacity, LANES)), jnp.int32),
            dma((6,)), dma((6,)), dma((n,)), dma((n,)), dma((n,)), dma((n,)),
        ],
        compiler_params=pltpu.CompilerParams(
            vmem_limit_bytes=53 << 20, collective_id=0, has_side_effects=True
        ),
    )(
        *(
            pltpu.with_memory_space_constraint(operand, pltpu.HBM)
            for operand in (
                temper, voxels, regular_window[None, :], shifted_window[None, :], dest[None, :], w_qkv, w_out, gain
            )
        )
    )


def solution(mesh):
    spread = P(("parts", "wide"))
    wide_rows = P(("parts", "wide"), None)
    return jax.shard_map(
        body,
        mesh=mesh,
        in_specs=(wide_rows, spread, spread, spread, P(), P(), P(), P()),
        out_specs=wide_rows,
        check_vma=False,
    )
```
